32 devices in a mesh: row: 4 (over x, core), col: 8 (over z, y).
Axes of the slice: x: 2, y: 2, z: 4, core: 2. Of those that a mesh axis runs over, the one named last changes fastest.
Arguments:
- corner: bfloat16 [25600, 25600], P('row', 'col'), may hold values from -32 to 32
- edge: bfloat16 [25600, 25600], P('row', 'col'), may hold values from -32 to 32
- sketch: bfloat16 [25600, 448], P('col'), may hold values from -6 to 6
Outputs:
- corner_new: float32 [400, 400], replicated
- edge_new: float32 [400, 400], replicated
The draws below stay inside these ranges and needn't reach their ends.
All inputs are finite; a program needn't handle non-finite values.
Results may differ from the reference program's by a relative error of at most 0.0015.
Values may be sent and summed in bfloat16 or wider, within the bound.
A program may use at most 256 MiB of HBM per device.

```python
import math
import jax
import jax.numpy as jnp
from jax import lax

CHI = 400
DD = 64
SKETCH = 448
RANK = 400
ORDER = 25600
N_ROW = 4


def dominant(key, shift, spread):
    order = CHI * DD
    noise = jax.random.normal(jax.random.fold_in(key, 23), (order, order), jnp.float32)
    matrix = shift * jnp.eye(order, dtype=jnp.float32) + spread / math.sqrt(order) * noise
    return matrix.astype(jnp.bfloat16)


def draw_corner(key, part):
    return dominant(jax.random.fold_in(key, 101), 3.0, 2.0)


def draw_edge(key, part):
    return dominant(jax.random.fold_in(key, 202), 2.0, 2.0)


def levels(own_key, shape, pieces, smallest, largest):
    def one(axis_at, shards_of):
        draws = jax.random.uniform(jax.random.fold_in(jax.random.fold_in(own_key, 6), axis_at), (shards_of,), jnp.float32, smallest / len(pieces), largest / len(pieces))
        return jnp.repeat(jnp.exp(draws), shape[axis_at] // shards_of).reshape((-1,) + (1,) * (len(shape) - axis_at - 1))

    loudness = one(*pieces[0])
    for cut in pieces[1:]:
        loudness = loudness * one(*cut)
    return loudness


def bell_draw(rng, extent, scale, reach, split=(), held_as=jnp.bfloat16):
    level = levels(rng, extent, split, -0.22, 0.18) if split else 1.0
    values = jax.random.normal(rng, extent, jnp.float32) * scale * level
    return jnp.minimum(jnp.maximum(values, -reach), reach).astype(held_as)


def setup_inputs(seed: int = 0) -> dict:
    streams_of = jax.random.split(jax.random.key(seed), 4)
    return {
        "corner": draw_corner(jax.random.fold_in(streams_of[3], 71), 0),
        "edge": draw_edge(jax.random.fold_in(streams_of[3], 71), 0),
        "sketch": bell_draw(streams_of[2], (ORDER, SKETCH), 1.0, 6.0, ((0, 8),)),
    }


def apply_blocks(matrix, right):
    blocks = matrix.reshape(N_ROW, ORDER // N_ROW, ORDER)
    result = lax.map(lambda block: jnp.dot(block.astype(jnp.float32), right.astype(jnp.float32), preferred_element_type=jnp.float32), blocks)
    return result.reshape(ORDER, right.shape[1])

def reference(corner, edge, sketch):
    sampled = apply_blocks(corner, sketch)
    gram = jnp.dot(sampled.T, sampled, precision=lax.Precision.HIGHEST)
    lower = jnp.linalg.cholesky(gram)
    basis = lax.linalg.triangular_solve(lower, sampled, left_side=False, lower=True, transpose_a=True)
    projector = basis[:, SKETCH - RANK:].astype(jnp.bfloat16)
    wide = projector.astype(jnp.float32)
    corner_image = apply_blocks(corner, projector)
    edge_image = apply_blocks(edge, projector)
    corner_new = jnp.dot(wide.T, corner_image, precision=lax.Precision.HIGHEST)
    edge_new = jnp.dot(wide.T, edge_image, precision=lax.Precision.HIGHEST)
    return (corner_new, edge_new)
```

```python
import jax
import jax.numpy as jnp
from jax import lax
from jax.sharding import PartitionSpec as P

RANK = 400
HIGHEST = lax.Precision.HIGHEST


def outer(left, right):
    return lax.dot_general(left, right, (((0,), (0,)), ((), ())), preferred_element_type=jnp.float32)


def exact_left(rows, image):
    upper_part = image.astype(jnp.bfloat16)
    lower_part = (image - upper_part.astype(jnp.float32)).astype(jnp.bfloat16)
    return outer(rows, upper_part) + outer(rows, lower_part)


def inverse_factor(gram):
    lower = jnp.linalg.cholesky(gram)
    unit = jnp.eye(gram.shape[0], dtype=gram.dtype)
    inverse = lax.linalg.triangular_solve(lower, unit, left_side=True, lower=True)
    return inverse[gram.shape[0] - RANK :]


def column_route(n_row, n_col):
    ratio = n_col // n_row
    route = []
    for source in range(n_row):
        for shard in range(n_col):
            half, target = divmod(shard, n_row)
            route.append((source * n_col + shard, target * n_col + source * ratio + half))
    return route


def body(corner, edge, sketch):
    n_row, n_col = lax.axis_size("row"), lax.axis_size("col")
    both = ("row", "col")
    part = jnp.dot(corner, sketch, preferred_element_type=jnp.float32).astype(jnp.bfloat16)
    shard = lax.psum_scatter(part, "col", scatter_dimension=0, tiled=True)
    gram = lax.psum(outer(shard, shard), both)
    moved = lax.ppermute(shard, both, column_route(n_row, n_col))
    cols = lax.all_gather(moved, "row", axis=0, tiled=True)
    rows = lax.all_gather(shard, "col", axis=0, tiled=True)
    inverse = inverse_factor(gram)

    def renormalize(matrix):
        image = jnp.dot(matrix, cols, preferred_element_type=jnp.float32)
        total = exact_left(rows, image)
        half = jnp.dot(inverse, total, precision=HIGHEST)
        return lax.dot_general(half, inverse, (((1,), (1,)), ((), ())), precision=HIGHEST)

    return lax.psum((renormalize(corner), renormalize(edge)), both)


def solution(mesh):
    placed = (P("row", "col"), P("row", "col"), P("col", None))
    return jax.shard_map(body, mesh=mesh, in_specs=placed, out_specs=(P(), P()), check_vma=False)
```

```python
import functools

import jax
import jax.numpy as jnp
from jax import lax
from jax.experimental import pallas as pl
from jax.experimental.pallas import tpu as pltpu
from jax.sharding import PartitionSpec as P

RANK = 400
HIGHEST = lax.Precision.HIGHEST
BLOCK = 128
TILE = 8
VMEM_LIMIT = 58 * 1024 * 1024


def outer(left, right, precision=None):
    return lax.dot_general(
        left, right, (((0,), (0,)), ((), ())), precision=precision, preferred_element_type=jnp.float32
    )


def row_tile(rows):
    for tile in (640, 512, 400, 320, 256, 160, 128, 64, 32, 16):
        if rows % tile == 0:
            return tile
    return rows


def sample_kernel(matrix, sketch, out):
    out[...] = jnp.dot(matrix[...], sketch[...], preferred_element_type=jnp.float32).astype(out.dtype)


def sample(matrix, sketch):
    rows, depth = matrix.shape
    width = sketch.shape[1]
    tile = row_tile(rows)
    return pl.pallas_call(
        sample_kernel,
        grid=(rows // tile,),
        out_shape=jax.ShapeDtypeStruct((rows, width), jnp.bfloat16),
        in_specs=[
            pl.BlockSpec((tile, depth), lambda i: (i, 0)),
            pl.BlockSpec((depth, width), lambda i: (0, 0)),
        ],
        out_specs=pl.BlockSpec((tile, width), lambda i: (i, 0)),
        compiler_params=pltpu.CompilerParams(vmem_limit_bytes=VMEM_LIMIT),
    )(matrix, sketch)


def pair_kernel(matrix, cols, rows, out):
    image = jnp.dot(matrix[...], cols[...], preferred_element_type=jnp.float32)
    upper_part = image.astype(jnp.bfloat16)
    lower_part = (image - upper_part.astype(jnp.float32)).astype(jnp.bfloat16)
    left = rows[...].T
    term = jnp.dot(left, upper_part, preferred_element_type=jnp.float32)
    term += jnp.dot(left, lower_part, preferred_element_type=jnp.float32)

    @pl.when(pl.program_id(0) == 0)
    def _():
        out[...] = term

    @pl.when(pl.program_id(0) > 0)
    def _():
        out[...] += term


def pair_product(matrix, cols, rows):
    height, depth = matrix.shape
    width = cols.shape[1]
    tile = row_tile(height)
    return pl.pallas_call(
        pair_kernel,
        grid=(height // tile,),
        out_shape=jax.ShapeDtypeStruct((width, width), jnp.float32),
        in_specs=[
            pl.BlockSpec((tile, depth), lambda i: (i, 0)),
            pl.BlockSpec((depth, width), lambda i: (0, 0)),
            pl.BlockSpec((tile, width), lambda i: (i, 0)),
        ],
        out_specs=pl.BlockSpec((width, width), lambda i: (0, 0)),
        compiler_params=pltpu.CompilerParams(vmem_limit_bytes=VMEM_LIMIT),
    )(matrix, cols, rows)


def eliminate(block):
    count = block.shape[0] // TILE
    row_ids = lax.broadcasted_iota(jnp.int32, (TILE, BLOCK), 0)
    lane_ids = lax.broadcasted_iota(jnp.int32, (TILE, BLOCK), 1)
    work = [block[t * TILE : (t + 1) * TILE, :] for t in range(count)]
    other = [(lane_ids == row_ids + t * TILE).astype(jnp.float32) for t in range(count)]
    for step in range(count * TILE):
        home, place = divmod(step, TILE)
        column = [jnp.broadcast_to(work[t][:, step : step + 1], (TILE, BLOCK)) for t in range(home, count)]
        scale = 1.0 / column[0][place : place + 1, :]
        pivot_row = work[home][place : place + 1, :] * scale
        other_row = other[home][place : place + 1, :] * scale
        for t in range(home, count):
            factor = column[t - home]
            if t == home:
                factor = jnp.where(row_ids > place, factor, 0.0)
            work[t] = work[t] - factor * pivot_row
            other[t] = other[t] - factor * other_row
    done = []
    for t in range(count):
        diagonal = jnp.sum(jnp.where(lane_ids == row_ids + t * TILE, work[t], 0.0), axis=1, keepdims=True)
        done.append(other[t] / jnp.sqrt(diagonal))
    return jnp.concatenate(done, axis=0)


def factor_kernel(gram, out, held):
    size = gram.shape[0]
    padded = held.shape[0]
    ids_r = lax.broadcasted_iota(jnp.int32, (padded, padded), 0)
    ids_c = lax.broadcasted_iota(jnp.int32, (padded, padded), 1)
    unit = (ids_r == ids_c).astype(jnp.float32)
    held[:, :padded] = unit
    held[:, padded:] = unit
    held[:size, :size] = gram[...]
    blocks = padded // BLOCK

    def one(k, carry):
        at = pl.multiple_of(k * BLOCK, BLOCK)
        inverse = eliminate(held[pl.ds(at, BLOCK), pl.ds(at, BLOCK)])
        strip = jnp.dot(inverse, held[pl.ds(at, BLOCK), :], precision=HIGHEST, preferred_element_type=jnp.float32)
        held[pl.ds(at, BLOCK), :] = strip

        def trail(i, inner):
            low = pl.multiple_of(i * BLOCK, BLOCK)
            side = held[pl.ds(at, BLOCK), pl.ds(low, BLOCK)]
            held[pl.ds(low, BLOCK), :] -= jnp.dot(
                side.T, held[pl.ds(at, BLOCK), :], precision=HIGHEST, preferred_element_type=jnp.float32
            )
            return inner

        lax.fori_loop(k + 1, blocks, trail, 0)
        return carry

    lax.fori_loop(0, blocks, one, 0)
    out[...] = held[:size, padded : padded + size]


def inverse_factor(gram):
    size = gram.shape[0]
    padded = -(-size // BLOCK) * BLOCK
    whole = pl.pallas_call(
        factor_kernel,
        out_shape=jax.ShapeDtypeStruct((size, size), jnp.float32),
        in_specs=[pl.BlockSpec(memory_space=pltpu.VMEM)],
        out_specs=pl.BlockSpec(memory_space=pltpu.VMEM),
        scratch_shapes=[pltpu.VMEM((padded, 2 * padded), jnp.float32)],
    )(gram)
    return whole[size - RANK :]


def reduce_kernel(n_row, n_col, x, out, row_land, col_land, part, total, *sems):
    send_a, recv_a, send_b, recv_b, send_c, recv_c, send_d, recv_d = sems
    me_row, me_col = lax.axis_index("row"), lax.axis_index("col")
    big = x.shape[0] // n_row
    small = big // n_col

    def peer(me, shift, count):
        return lax.rem(me + shift, count)

    def row_of(shift):
        return (peer(me_row, shift, n_row), me_col)

    def col_of(shift):
        return (me_row, peer(me_col, shift, n_col))

    def copy(source, target, send, recv, device):
        return pltpu.make_async_remote_copy(
            src_ref=source, dst_ref=target, send_sem=send, recv_sem=recv,
            device_id=device, device_id_type=pl.DeviceIdType.MESH,
        )

    def at(index, size):
        return pl.ds(pl.multiple_of(index * size, TILE), size)

    barrier = pltpu.get_barrier_semaphore()
    for d in range(1, n_row):
        pl.semaphore_signal(barrier, inc=1, device_id=row_of(d), device_id_type=pl.DeviceIdType.MESH)
    for d in range(1, n_col):
        pl.semaphore_signal(barrier, inc=1, device_id=col_of(d), device_id_type=pl.DeviceIdType.MESH)
    pl.semaphore_wait(barrier, n_row + n_col - 2)

    first = []
    for d in range(1, n_row):
        chunk = x.at[at(peer(me_row, d, n_row), big), :]
        first.append(copy(chunk, row_land.at[d - 1], send_a.at[d - 1], recv_a.at[d - 1], row_of(d)))
        first[-1].start()
    summed = x[at(me_row, big), :]
    for d in range(1, n_row):
        first[d - 1].wait_recv()
        summed += row_land[d - 1]
    part[...] = summed

    second = []
    for d in range(1, n_col):
        chunk = part.at[at(peer(me_col, d, n_col), small), :]
        second.append(copy(chunk, col_land.at[d - 1], send_b.at[d - 1], recv_b.at[d - 1], col_of(d)))
        second[-1].start()
    summed = part[at(me_col, small), :]
    for d in range(1, n_col):
        second[d - 1].wait_recv()
        summed += col_land[d - 1]
    total[...] = summed

    mine = pl.ds(pl.multiple_of(me_row * big + me_col * small, TILE), small)
    third = []
    for d in range(1, n_col):
        third.append(copy(total, out.at[mine, :], send_c.at[d - 1], recv_c.at[d - 1], col_of(d)))
        third[-1].start()
    out[mine, :] = summed
    for d in range(1, n_col):
        third[d - 1].wait_recv()

    fourth = []
    for d in range(1, n_row):
        chunk = out.at[at(me_row, big), :]
        fourth.append(copy(chunk, chunk, send_d.at[d - 1], recv_d.at[d - 1], row_of(d)))
        fourth[-1].start()
    for d in range(1, n_row):
        fourth[d - 1].wait_recv()
    for sent in first + second + third + fourth:
        sent.wait_send()


def reduce_all(value, collective_id):
    n_row, n_col = lax.axis_size("row"), lax.axis_size("col")
    height, width = value.shape
    grain = n_row * n_col * TILE
    padded = -(-height // grain) * grain
    value = jnp.pad(value, ((0, padded - height), (0, 0)))
    big = padded // n_row
    small = big // n_col
    dma = pltpu.SemaphoreType.DMA
    result = pl.pallas_call(
        functools.partial(reduce_kernel, n_row, n_col),
        out_shape=jax.ShapeDtypeStruct((padded, width), jnp.float32),
        in_specs=[pl.BlockSpec(memory_space=pltpu.VMEM)],
        out_specs=pl.BlockSpec(memory_space=pltpu.VMEM),
        scratch_shapes=[
            pltpu.VMEM((n_row - 1, big, width), jnp.float32),
            pltpu.VMEM((n_col - 1, small, width), jnp.float32),
            pltpu.VMEM((big, width), jnp.float32),
            pltpu.VMEM((small, width), jnp.float32),
        ]
        + [dma((n_row - 1,)), dma((n_row - 1,)), dma((n_col - 1,)), dma((n_col - 1,))]
        + [dma((n_col - 1,)), dma((n_col - 1,)), dma((n_row - 1,)), dma((n_row - 1,))],
        compiler_params=pltpu.CompilerParams(collective_id=collective_id, has_side_effects=True),
    )(value)
    return result[:height]


def column_route(n_row, n_col):
    ratio = n_col // n_row
    route = []
    for source in range(n_row):
        for shard in range(n_col):
            half, target = divmod(shard, n_row)
            route.append((source * n_col + shard, target * n_col + source * ratio + half))
    return route


def body(corner, edge, sketch):
    n_row, n_col = lax.axis_size("row"), lax.axis_size("col")
    both = ("row", "col")
    shard = lax.psum_scatter(sample(corner, sketch), "col", scatter_dimension=0, tiled=True)
    moved = lax.ppermute(shard, both, column_route(n_row, n_col))
    cols = lax.all_gather(moved, "row", axis=0, tiled=True)
    rows = lax.all_gather(shard, "col", axis=0, tiled=True)
    gram = reduce_all(outer(shard, shard), 0)
    inverse = inverse_factor(gram)

    def renormalize(matrix):
        total = pair_product(matrix, cols, rows)
        half = jnp.dot(inverse, total, precision=HIGHEST)
        return lax.dot_general(half, inverse, (((1,), (1,)), ((), ())), precision=HIGHEST)

    stacked = jnp.concatenate([renormalize(corner), renormalize(edge)], axis=0)
    result = reduce_all(stacked, 1)
    return result[:RANK], result[RANK:]


def solution(mesh):
    placed = (P("row", "col"), P("row", "col"), P("col", None))
    return jax.shard_map(body, mesh=mesh, in_specs=placed, out_specs=(P(), P()), check_vma=False)
```

```python
import functools

import jax
import jax.numpy as jnp
from jax import lax
from jax.experimental import pallas as pl
from jax.experimental.pallas import tpu as pltpu
from jax.sharding import PartitionSpec as P

RANK = 400
HIGHEST = lax.Precision.HIGHEST
BLOCK = 128
TILE = 8
VMEM_LIMIT = 58 * 1024 * 1024


def outer(left, right, precision=None):
    return lax.dot_general(
        left, right, (((0,), (0,)), ((), ())), precision=precision, preferred_element_type=jnp.float32
    )


def row_tile(rows):
    for tile in (640, 512, 400, 320, 256, 160, 128, 64, 32, 16):
        if rows % tile == 0:
            return tile
    return rows


def sample_kernel(matrix, sketch, out):
    out[...] = jnp.dot(matrix[...], sketch[...], preferred_element_type=jnp.float32).astype(out.dtype)


def sample(matrix, sketch):
    rows, depth = matrix.shape
    width = sketch.shape[1]
    tile = row_tile(rows)
    return pl.pallas_call(
        sample_kernel,
        grid=(rows // tile,),
        out_shape=jax.ShapeDtypeStruct((rows, width), jnp.bfloat16),
        in_specs=[
            pl.BlockSpec((tile, depth), lambda i: (i, 0)),
            pl.BlockSpec((depth, width), lambda i: (0, 0)),
        ],
        out_specs=pl.BlockSpec((tile, width), lambda i: (i, 0)),
        compiler_params=pltpu.CompilerParams(vmem_limit_bytes=VMEM_LIMIT),
    )(matrix, sketch)


def image_kernel(matrix, cols, out):
    out[...] = jnp.dot(matrix[...], cols[...], preferred_element_type=jnp.float32)


def image_of(matrix, cols):
    height, depth = matrix.shape
    width = cols.shape[1]
    tile = row_tile(height)
    return pl.pallas_call(
        image_kernel,
        grid=(height // tile,),
        out_shape=jax.ShapeDtypeStruct((height, width), jnp.float32),
        in_specs=[
            pl.BlockSpec((tile, depth), lambda i: (i, 0)),
            pl.BlockSpec((depth, width), lambda i: (0, 0)),
        ],
        out_specs=pl.BlockSpec((tile, width), lambda i: (i, 0)),
        cost_estimate=pl.CostEstimate(
            flops=2 * height * depth * width, bytes_accessed=2 * height * depth, transcendentals=0
        ),
        compiler_params=pltpu.CompilerParams(vmem_limit_bytes=VMEM_LIMIT),
    )(matrix, cols)


def left_kernel(rows, first, second, first_out, second_out):
    left = rows[...].T

    def term(image):
        upper_part = image.astype(jnp.bfloat16)
        lower_part = (image - upper_part.astype(jnp.float32)).astype(jnp.bfloat16)
        found = jnp.dot(left, upper_part, preferred_element_type=jnp.float32)
        return found + jnp.dot(left, lower_part, preferred_element_type=jnp.float32)

    @pl.when(pl.program_id(0) == 0)
    def _():
        first_out[...] = jnp.zeros_like(first_out)
        second_out[...] = jnp.zeros_like(second_out)

    first_out[...] += term(first[...])
    second_out[...] += term(second[...])


def left_products(rows, first, second):
    height, width = rows.shape
    tile = row_tile(height)
    tall = pl.BlockSpec((tile, width), lambda i: (i, 0))
    square = pl.BlockSpec((width, width), lambda i: (0, 0))
    shape = jax.ShapeDtypeStruct((width, width), jnp.float32)
    return pl.pallas_call(
        left_kernel,
        grid=(height // tile,),
        out_shape=(shape, shape),
        in_specs=[tall, tall, tall],
        out_specs=(square, square),
        compiler_params=pltpu.CompilerParams(vmem_limit_bytes=VMEM_LIMIT),
    )(rows, first, second)


def eliminate(block):
    count = block.shape[0] // TILE
    row_ids = lax.broadcasted_iota(jnp.int32, (TILE, BLOCK), 0)
    lane_ids = lax.broadcasted_iota(jnp.int32, (TILE, BLOCK), 1)
    work = [block[t * TILE : (t + 1) * TILE, :] for t in range(count)]
    other = [(lane_ids == row_ids + t * TILE).astype(jnp.float32) for t in range(count)]
    for step in range(count * TILE):
        home, place = divmod(step, TILE)
        column = [jnp.broadcast_to(work[t][:, step : step + 1], (TILE, BLOCK)) for t in range(home, count)]
        scale = 1.0 / column[0][place : place + 1, :]
        pivot_row = work[home][place : place + 1, :] * scale
        other_row = other[home][place : place + 1, :] * scale
        for t in range(home, count):
            factor = column[t - home]
            if t == home:
                factor = jnp.where(row_ids > place, factor, 0.0)
            work[t] = work[t] - factor * pivot_row
            other[t] = other[t] - factor * other_row
    done = []
    for t in range(count):
        diagonal = jnp.sum(jnp.where(lane_ids == row_ids + t * TILE, work[t], 0.0), axis=1, keepdims=True)
        done.append(other[t] / jnp.sqrt(diagonal))
    return jnp.concatenate(done, axis=0)


def factor_kernel(gram, out, held):
    size = gram.shape[0]
    padded = held.shape[0]
    ids_r = lax.broadcasted_iota(jnp.int32, (padded, padded), 0)
    ids_c = lax.broadcasted_iota(jnp.int32, (padded, padded), 1)
    unit = (ids_r == ids_c).astype(jnp.float32)
    held[:, :padded] = unit
    held[:, padded:] = unit
    held[:size, :size] = gram[...]
    blocks = padded // BLOCK

    def one(k, carry):
        at = pl.multiple_of(k * BLOCK, BLOCK)
        inverse = eliminate(held[pl.ds(at, BLOCK), pl.ds(at, BLOCK)])
        strip = jnp.dot(inverse, held[pl.ds(at, BLOCK), :], precision=HIGHEST, preferred_element_type=jnp.float32)
        held[pl.ds(at, BLOCK), :] = strip

        def trail(i, inner):
            low = pl.multiple_of(i * BLOCK, BLOCK)
            side = held[pl.ds(at, BLOCK), pl.ds(low, BLOCK)]
            held[pl.ds(low, BLOCK), :] -= jnp.dot(
                side.T, held[pl.ds(at, BLOCK), :], precision=HIGHEST, preferred_element_type=jnp.float32
            )
            return inner

        lax.fori_loop(k + 1, blocks, trail, 0)
        return carry

    lax.fori_loop(0, blocks, one, 0)
    out[...] = held[:size, padded : padded + size]


def inverse_factor(gram):
    size = gram.shape[0]
    padded = -(-size // BLOCK) * BLOCK
    whole = pl.pallas_call(
        factor_kernel,
        out_shape=jax.ShapeDtypeStruct((size, size), jnp.float32),
        in_specs=[pl.BlockSpec(memory_space=pltpu.VMEM)],
        out_specs=pl.BlockSpec(memory_space=pltpu.VMEM),
        scratch_shapes=[pltpu.VMEM((padded, 2 * padded), jnp.float32)],
        cost_estimate=pl.CostEstimate(
            flops=100 * padded * padded * padded, bytes_accessed=8 * size * size, transcendentals=0
        ),
    )(gram)
    return whole[size - RANK :]


def reduce_kernel(n_row, n_col, x, out, row_land, col_land, part, total, *sems):
    send_a, recv_a, send_b, recv_b, send_c, recv_c, send_d, recv_d = sems
    me_row, me_col = lax.axis_index("row"), lax.axis_index("col")
    big = x.shape[0] // n_row
    small = big // n_col

    def peer(me, shift, count):
        return lax.rem(me + shift, count)

    def row_of(shift):
        return (peer(me_row, shift, n_row), me_col)

    def col_of(shift):
        return (me_row, peer(me_col, shift, n_col))

    def copy(source, target, send, recv, device):
        return pltpu.make_async_remote_copy(
            src_ref=source, dst_ref=target, send_sem=send, recv_sem=recv,
            device_id=device, device_id_type=pl.DeviceIdType.MESH,
        )

    def at(index, size):
        return pl.ds(pl.multiple_of(index * size, TILE), size)

    barrier = pltpu.get_barrier_semaphore()
    for d in range(1, n_row):
        pl.semaphore_signal(barrier, inc=1, device_id=row_of(d), device_id_type=pl.DeviceIdType.MESH)
    for d in range(1, n_col):
        pl.semaphore_signal(barrier, inc=1, device_id=col_of(d), device_id_type=pl.DeviceIdType.MESH)
    pl.semaphore_wait(barrier, n_row + n_col - 2)

    first = []
    for d in range(1, n_row):
        chunk = x.at[at(peer(me_row, d, n_row), big), :]
        first.append(copy(chunk, row_land.at[d - 1], send_a.at[d - 1], recv_a.at[d - 1], row_of(d)))
        first[-1].start()
    summed = x[at(me_row, big), :]
    for d in range(1, n_row):
        first[d - 1].wait_recv()
        summed += row_land[d - 1]
    part[...] = summed

    second = []
    for d in range(1, n_col):
        chunk = part.at[at(peer(me_col, d, n_col), small), :]
        second.append(copy(chunk, col_land.at[d - 1], send_b.at[d - 1], recv_b.at[d - 1], col_of(d)))
        second[-1].start()
    summed = part[at(me_col, small), :]
    for d in range(1, n_col):
        second[d - 1].wait_recv()
        summed += col_land[d - 1]
    total[...] = summed

    mine = pl.ds(pl.multiple_of(me_row * big + me_col * small, TILE), small)
    third = []
    for d in range(1, n_col):
        third.append(copy(total, out.at[mine, :], send_c.at[d - 1], recv_c.at[d - 1], col_of(d)))
        third[-1].start()
    out[mine, :] = summed
    for d in range(1, n_col):
        third[d - 1].wait_recv()

    fourth = []
    for d in range(1, n_row):
        chunk = out.at[at(me_row, big), :]
        fourth.append(copy(chunk, chunk, send_d.at[d - 1], recv_d.at[d - 1], row_of(d)))
        fourth[-1].start()
    for d in range(1, n_row):
        fourth[d - 1].wait_recv()
    for sent in first + second + third + fourth:
        sent.wait_send()


def reduce_all(value, collective_id):
    n_row, n_col = lax.axis_size("row"), lax.axis_size("col")
    height, width = value.shape
    grain = n_row * n_col * TILE
    padded = -(-height // grain) * grain
    value = jnp.pad(value, ((0, padded - height), (0, 0)))
    big = padded // n_row
    small = big // n_col
    dma = pltpu.SemaphoreType.DMA
    result = pl.pallas_call(
        functools.partial(reduce_kernel, n_row, n_col),
        out_shape=jax.ShapeDtypeStruct((padded, width), jnp.float32),
        in_specs=[pl.BlockSpec(memory_space=pltpu.VMEM)],
        out_specs=pl.BlockSpec(memory_space=pltpu.VMEM),
        scratch_shapes=[
            pltpu.VMEM((n_row - 1, big, width), jnp.float32),
            pltpu.VMEM((n_col - 1, small, width), jnp.float32),
            pltpu.VMEM((big, width), jnp.float32),
            pltpu.VMEM((small, width), jnp.float32),
        ]
        + [dma((n_row - 1,)), dma((n_row - 1,)), dma((n_col - 1,)), dma((n_col - 1,))]
        + [dma((n_col - 1,)), dma((n_col - 1,)), dma((n_row - 1,)), dma((n_row - 1,))],
        compiler_params=pltpu.CompilerParams(collective_id=collective_id, has_side_effects=True),
    )(value)
    return result[:height]


def column_route(n_row, n_col):
    ratio = n_col // n_row
    route = []
    for source in range(n_row):
        for shard in range(n_col):
            half, target = divmod(shard, n_row)
            route.append((source * n_col + shard, target * n_col + source * ratio + half))
    return route


def body(corner, edge, sketch):
    n_row, n_col = lax.axis_size("row"), lax.axis_size("col")
    both = ("row", "col")
    shard = lax.psum_scatter(sample(corner, sketch), "col", scatter_dimension=0, tiled=True)
    gram = reduce_all(outer(shard, shard), 0)
    shard, gram = lax.optimization_barrier((shard, gram))
    moved = lax.ppermute(shard, both, column_route(n_row, n_col))
    cols = lax.all_gather(moved, "row", axis=0, tiled=True)
    rows = lax.all_gather(shard, "col", axis=0, tiled=True)
    inverse = inverse_factor(gram)
    corner_image, edge_image = image_of(corner, cols), image_of(edge, cols)

    def renormalize(total):
        half = jnp.dot(inverse, total, precision=HIGHEST)
        return lax.dot_general(half, inverse, (((1,), (1,)), ((), ())), precision=HIGHEST)

    corner_sum, edge_sum = left_products(rows, corner_image, edge_image)
    stacked = jnp.concatenate([renormalize(corner_sum), renormalize(edge_sum)], axis=0)
    result = reduce_all(stacked, 1)
    return result[:RANK], result[RANK:]


def solution(mesh):
    placed = (P("row", "col"), P("row", "col"), P("col", None))
    return jax.shard_map(body, mesh=mesh, in_specs=placed, out_specs=(P(), P()), check_vma=False)
```
